32 devices in a mesh: space: 16 (over z, x, core), chan: 2 (over y).
Axes of the slice: x: 2, y: 2, z: 4, core: 2. Of those that a mesh axis runs over, the one named last changes fastest.
Arguments:
- volume: bfloat16 [256, 16, 8, 128], P('chan', 'space'), may hold values from -6 to 6
- w_first: bfloat16 [256, 27, 256], P(None, None, 'chan'), may hold values from -0.078125 to 0.078125
- b_first: float32 [256], P('chan'), may hold values from -1.8 to 1.8
- w_second: bfloat16 [256, 27, 256], P('chan'), may hold values from -0.125 to 0.125
- b_second: float32 [256], P('chan'), may hold values from -1.8 to 1.8
Outputs:
- result: bfloat16 [256, 16, 8, 128], P('chan', 'space')
The draws below stay inside these ranges and needn't reach their ends.
All inputs are finite; a program needn't handle non-finite values.
Results may differ from the reference program's by a relative error of at most 0.011.
Values may be sent and summed in bfloat16 or wider, within the bound.
No kernel may reach another device: no remote copies, remote signals or barrier semaphores. Data moves between devices by JAX's collectives and lax.ppermute only.
A program may use at most 64 MiB of HBM per device.

```python
import jax
import jax.numpy as jnp
from jax import lax

C = 256
H = 8
W = 128
DEPTH = 16


def spiked(result, stream_key, source, target, shards_of, factor):
    def block_of(position):
        return (jnp.arange(result.shape[position]) // (result.shape[position] // shards_of)).reshape((-1,) + (1,) * (result.ndim - 1 - position))

    first = jax.random.permutation(stream_key, shards_of)[block_of(target)]
    far = (block_of(target) + shards_of // 2) % shards_of
    return jnp.where((block_of(source) == first) | (block_of(source) == far), factor * result, result)


def levels(stream_key, extent, pieces, low, top_value):
    def one(position, shards_of):
        heights = jax.random.uniform(jax.random.fold_in(jax.random.fold_in(stream_key, 6), position), (shards_of,), jnp.float32, low / len(pieces), top_value / len(pieces))
        return jnp.repeat(jnp.exp(heights), extent[position] // shards_of).reshape((-1,) + (1,) * (len(extent) - position - 1))

    loudness = one(*pieces[0])
    for cut in pieces[1:]:
        loudness = loudness * one(*cut)
    return loudness


def scatter_about(key, shape, width, most, split=(), dtype=jnp.bfloat16):
    level = levels(key, shape, split, -0.22, 0.18) if split else 1.0
    array = jax.random.normal(key, shape, jnp.float32) * width * level
    return jnp.minimum(jnp.maximum(array, -most), most).astype(dtype)


def bell_draw_with(rng, extent, width, bound, cuts, heavy, kind=jnp.bfloat16):
    array = width * jax.random.normal(rng, extent, jnp.float32)
    if cuts:
        array = array * levels(rng, extent, cuts, -0.22, 0.18)
    return jnp.clip(spiked(array, jax.random.fold_in(rng, 3), *heavy), -bound, bound).astype(kind)


def setup_inputs(seed: int = 0) -> dict:
    key_of = jax.random.split(jax.random.key(seed), 6)
    volume = scatter_about(key_of[0], (C, DEPTH, H, W), 1.0, 6.0, ((0, 2), (1, 16)))
    w_first = scatter_about(key_of[1], (C, 27, C), (27 * C) ** -0.5, 0.078125, ((2, 2),))
    b_first = scatter_about(key_of[2], (C,), 0.3, 1.8, ((0, 2),), jnp.float32)
    w_second = bell_draw_with(key_of[3], (C, 27, C), (27 * C // 2) ** -0.5, 0.125, ((0, 2),), (0, 2, 2, 2.0))
    b_second = scatter_about(key_of[4], (C,), 0.3, 1.8, ((0, 2),), jnp.float32)
    return dict(volume=volume, w_first=w_first, b_first=b_first, w_second=w_second, b_second=b_second)


def convolve(volume, weights, bias):
    kernel = weights.astype(jnp.float32).reshape(weights.shape[0], 3, 3, 3, weights.shape[2])
    summed = lax.conv_general_dilated(volume.astype(jnp.float32)[None], kernel, (1, 1, 1), "SAME", dimension_numbers=("NCDHW", "IDHWO", "NCDHW"), precision=lax.Precision.HIGHEST)[0]
    return jax.nn.relu(summed + bias[:, None, None, None]).astype(jnp.bfloat16)


def reference(volume, w_first, b_first, w_second, b_second):
    hidden = convolve(volume, w_first, b_first)
    return convolve(hidden, w_second, b_second)
```

```python
import functools

import jax
import jax.numpy as jnp
from jax import lax
from jax.experimental import pallas as pl
from jax.experimental.pallas import tpu as pltpu
from jax.sharding import PartitionSpec as P

F32 = jnp.float32
BF16 = jnp.bfloat16
VMEM_LIMIT = 20 << 20


def sds(shape, dtype):
    return jax.ShapeDtypeStruct(shape, dtype)


def run(kernel, outs, args, scratch=(), flops=0):
    moved = sum(a.size * a.dtype.itemsize for a in args)
    return pl.pallas_call(
        kernel,
        out_shape=outs,
        scratch_shapes=scratch,
        compiler_params=pltpu.CompilerParams(vmem_limit_bytes=VMEM_LIMIT),
        cost_estimate=pl.CostEstimate(
            flops=flops, bytes_accessed=moved, transcendentals=0
        ),
    )(*args)


def rows_last(block):
    c, h, w = block.shape
    planes = jnp.transpose(block, (1, 0, 2))
    return jnp.concatenate([planes[i].T for i in range(h)], axis=0).astype(F32)


def channels_first(cells, h, w):
    planes = jnp.stack([cells[i * w : (i + 1) * w].T for i in range(h)])
    return jnp.transpose(planes, (1, 0, 2))


def lay_columns(cells, framed, h, w):
    c = cells.shape[1]
    hw = h * w
    column = lax.broadcasted_iota(jnp.int32, (hw, 1), 0) % w
    left = jnp.where(column == 0, 0.0, pltpu.roll(cells, 1, 0))
    right = jnp.where(column == w - 1, 0.0, pltpu.roll(cells, hw - 1, 0))
    blank = jnp.zeros((w, 3 * c), BF16)
    framed[0:w] = blank
    framed[w + hw : 2 * w + hw] = blank
    framed[w : w + hw, 0:c] = left.astype(BF16)
    framed[w : w + hw, c : 2 * c] = cells.astype(BF16)
    framed[w : w + hw, 2 * c : 3 * c] = right.astype(BF16)


def nine_taps(framed, weights, h, w):
    hw = h * w
    _, c, n = weights.shape
    if c % 128 == 0:
        lhs = jnp.concatenate([framed[b * w : b * w + hw] for b in range(3)], axis=1)
        return jnp.dot(lhs, weights.reshape(9 * c, n), preferred_element_type=F32)
    total = None
    for b in range(3):
        term = jnp.dot(
            framed[b * w : b * w + hw],
            weights[3 * b : 3 * b + 3].reshape(3 * c, n),
            preferred_element_type=F32,
        )
        total = term if total is None else total + term
    return total


def depth_taps(where, weights, rows=None):
    return weights[pl.ds(where * 9, 9)] if rows is None else weights[pl.ds(where * 9, 9), rows]


def per_device(ns, nc, volume, w_first, b_first, w_second, b_second):
    cb, _, h, w = volume.shape
    hw = h * w
    ob = w_first.shape[2]
    full = w_second.shape[2]
    own_out = full // nc
    framed_in = sds(((h + 2) * w, 3 * cb), BF16)
    framed_mid = sds(((h + 2) * w, 3 * ob), BF16)
    volume = volume.reshape(cb, h, w)
    w_first = jnp.transpose(w_first, (1, 0, 2))
    w_second = jnp.transpose(w_second, (1, 0, 2))
    b_first = b_first.reshape(1, ob)
    b_second = b_second.reshape(own_out, 1, 1)

    pairs = [(i, i ^ 1) for i in range(ns)]
    beside = [(i, i + 1) for i in range(1, ns - 1, 2)]
    beside = beside + [(j, i) for i, j in beside]
    in_chip = lambda x: lax.ppermute(x, "space", pairs)
    next_chip = lambda x: lax.ppermute(x, "space", beside)
    round_chan = lambda x, k: lax.ppermute(
        x, "chan", [(i, (i + k) % nc) for i in range(nc)]
    )

    def odd():
        return lax.rem(lax.axis_index("space"), 2)

    def chan_rows(k, size):
        owner = lax.rem(lax.axis_index("chan") + nc - k, nc)
        return pl.ds(pl.multiple_of(owner * size, size), size)

    to_pair = lambda: 2 * odd()
    to_next = lambda: 2 - 2 * odd()

    def first_own(vol, wt, next_ref, pair_ref, mid_ref, framed):
        lay_columns(rows_last(vol[...]), framed, h, w)
        block = chan_rows(0, cb)
        next_ref[...] = nine_taps(framed, depth_taps(to_next(), wt, block), h, w)
        pair_ref[...] = nine_taps(framed, depth_taps(to_pair(), wt, block), h, w)
        mid_ref[...] = nine_taps(framed, depth_taps(1, wt, block), h, w)

    part = sds((hw, ob), F32)
    half = sds((hw, ob), BF16)
    arrived = [round_chan(volume, k) for k in range(1, nc)]
    own_next, own_pair, own_mid = run(
        first_own,
        [part, part, part],
        (volume, w_first),
        [pltpu.VMEM(framed_in.shape, BF16)],
        flops=54 * hw * cb * ob,
    )

    def first_sides(*refs):
        vols, (wt, next_ref, pair_ref) = refs[: nc - 1], refs[nc - 1 : nc + 2]
        to_next_ref, to_pair_ref = refs[nc + 2 : nc + 4]
        frames = refs[nc + 4 :]
        onward, across = next_ref[...], pair_ref[...]
        for k in range(1, nc):
            lay_columns(rows_last(vols[k - 1][...]), frames[k - 1], h, w)
            block = chan_rows(k, cb)
            onward += nine_taps(frames[k - 1], depth_taps(to_next(), wt, block), h, w)
            across += nine_taps(frames[k - 1], depth_taps(to_pair(), wt, block), h, w)
        to_next_ref[...] = onward.astype(BF16)
        to_pair_ref[...] = across.astype(BF16)

    to_next_part, to_pair_part, *frames = run(
        first_sides,
        [half, half] + [framed_in] * (nc - 1),
        (*arrived, w_first, own_next, own_pair),
        flops=36 * hw * cb * ob * (nc - 1),
    )
    pair_part = in_chip(to_pair_part)
    next_part = next_chip(to_next_part)

    def first_mid(*refs):
        blocks, (wt, mid_ref, pair_ref, sum_ref, edge_ref) = refs[: nc - 1], refs[nc - 1 :]
        total = mid_ref[...] + pair_ref[...].astype(F32)
        for k in range(1, nc):
            taps = depth_taps(1, wt, chan_rows(k, cb))
            total += nine_taps(blocks[k - 1], taps, h, w)
        sum_ref[...] = total
        edge_ref[...] = total.astype(BF16)

    so_far, edge_sum = run(
        first_mid,
        [part, half],
        (*frames, w_first, own_mid, pair_part),
        flops=18 * hw * cb * ob * (nc - 1),
    )
    next_edge = next_chip(edge_sum)

    def hidden_own(sum_ref, side_ref, b, out):
        total = sum_ref[...] + side_ref[...].astype(F32) + b[...]
        out[...] = jnp.maximum(total, 0.0).astype(BF16)

    hidden = run(hidden_own, half, (so_far, next_part, b_first), flops=3 * hw * ob)
    pair_hidden = in_chip(hidden)

    def second_own(cells, wt, out, framed):
        lay_columns(cells[...].astype(F32), framed, h, w)
        out[...] = nine_taps(framed, depth_taps(1, wt), h, w)

    def second_pair(cells, wt, before, out, framed):
        lay_columns(cells[...].astype(F32), framed, h, w)
        out[...] = before[...] + nine_taps(framed, depth_taps(2 - 2 * odd(), wt), h, w)

    scratch_mid = [pltpu.VMEM(framed_mid.shape, BF16)]
    whole = sds((hw, full), F32)
    second = run(second_own, whole, (hidden, w_second), scratch_mid, 18 * hw * ob * full)
    second = run(
        second_pair, whole, (pair_hidden, w_second, second), scratch_mid, 18 * hw * ob * full
    )

    def wanted(k):
        owner = lax.rem(lax.axis_index("chan") + k, nc)
        return pl.ds(pl.multiple_of(owner * own_out, own_out), own_out)

    def taps_for(wt, where, k):
        if own_out % 128 == 0:
            return wt[pl.ds(where * 9, 9), :, wanted(k)]
        owner = lax.rem(lax.axis_index("chan") + k, nc)
        taps = wt[pl.ds(where * 9, 9)]
        picked = taps[:, :, 0:own_out]
        for i in range(1, nc):
            picked = jnp.where(owner == i, taps[:, :, i * own_out : (i + 1) * own_out], picked)
        return picked

    def columns_for(ref, k):
        if own_out % 128 == 0:
            return ref[:, wanted(k)]
        owner = lax.rem(lax.axis_index("chan") + k, nc)
        cells = ref[...]
        picked = cells[:, 0:own_out]
        for i in range(1, nc):
            picked = jnp.where(owner == i, cells[:, i * own_out : (i + 1) * own_out], picked)
        return picked

    def second_send(edge_ref, mine_ref, b, wt, before, *refs):
        outs, framed = refs[:-1], refs[-1]
        place = lax.axis_index("space")
        inside = jnp.logical_and(place > 0, place < ns - 1)
        total = edge_ref[...].astype(F32) + mine_ref[...].astype(F32) + b[...]
        cells = jnp.where(inside, jnp.maximum(total, 0.0), 0.0)
        lay_columns(cells, framed, h, w)
        for k in range(1, nc):
            taps = taps_for(wt, 2 * odd(), k)
            sums = columns_for(before, k) + nine_taps(framed, taps, h, w)
            outs[k - 1][...] = channels_first(sums, h, w).astype(BF16)

    *sends, framed_edge = run(
        second_send,
        [sds((own_out, h, w), BF16)] * (nc - 1) + [framed_mid],
        (next_edge, to_next_part, b_first, w_second, second),
        flops=18 * hw * ob * own_out * (nc - 1),
    )
    parts = [round_chan(sends[k - 1], k) for k in range(1, nc)]

    def second_keep(framed, wt, before, b, out):
        taps = taps_for(wt, 2 * odd(), 0)
        sums = columns_for(before, 0) + nine_taps(framed, taps, h, w)
        out[...] = channels_first(sums, h, w) + b[...]

    kept = run(
        second_keep,
        sds((own_out, h, w), F32),
        (framed_edge, w_second, second, b_second),
        flops=18 * hw * ob * own_out,
    )

    def finish(kept_ref, *refs):
        total = kept_ref[...]
        for ref in refs[:-1]:
            total += ref[...].astype(F32)
        refs[-1][...] = jnp.maximum(total, 0.0).astype(BF16)

    result = run(finish, sds((own_out, h, w), BF16), (kept, *parts), flops=2 * hw * own_out)
    return result.reshape(own_out, 1, h, w)


def solution(mesh):
    in_specs = (
        P("chan", "space", None, None),
        P(None, None, "chan"),
        P("chan"),
        P("chan", None, None),
        P("chan"),
    )
    return jax.shard_map(
        functools.partial(per_device, mesh.shape["space"], mesh.shape["chan"]),
        mesh=mesh,
        in_specs=in_specs,
        out_specs=P("chan", "space", None, None),
        check_vma=False,
    )
```

```python
import functools

import jax
import jax.numpy as jnp
from jax import lax
from jax.experimental import pallas as pl
from jax.experimental.pallas import tpu as pltpu
from jax.sharding import PartitionSpec as P

F32 = jnp.float32
BF16 = jnp.bfloat16
VMEM_LIMIT = 20 << 20


def sds(shape, dtype):
    return jax.ShapeDtypeStruct(shape, dtype)


def run(kernel, outs, args, scratch=(), flops=0):
    moved = sum(a.size * a.dtype.itemsize for a in args) if flops else 0
    return pl.pallas_call(
        kernel,
        out_shape=outs,
        scratch_shapes=scratch,
        compiler_params=pltpu.CompilerParams(vmem_limit_bytes=VMEM_LIMIT),
        cost_estimate=pl.CostEstimate(
            flops=flops, bytes_accessed=moved, transcendentals=0
        ),
    )(*args)


def rows_last(block):
    c, h, w = block.shape
    planes = jnp.transpose(block, (1, 0, 2))
    return jnp.concatenate([planes[i].T for i in range(h)], axis=0).astype(F32)


def channels_first(cells, h, w):
    planes = jnp.stack([cells[i * w : (i + 1) * w].T for i in range(h)])
    return jnp.transpose(planes, (1, 0, 2))


def lay_columns(cells, framed, h, w):
    c = cells.shape[1]
    hw = h * w
    column = lax.broadcasted_iota(jnp.int32, (hw, 1), 0) % w
    left = jnp.where(column == 0, 0.0, pltpu.roll(cells, 1, 0))
    right = jnp.where(column == w - 1, 0.0, pltpu.roll(cells, hw - 1, 0))
    blank = jnp.zeros((w, 3 * c), BF16)
    framed[0:w] = blank
    framed[w + hw : 2 * w + hw] = blank
    framed[w : w + hw, 0:c] = left.astype(BF16)
    framed[w : w + hw, c : 2 * c] = cells.astype(BF16)
    framed[w : w + hw, 2 * c : 3 * c] = right.astype(BF16)


def nine_taps(framed, weights, h, w):
    hw = h * w
    _, c, n = weights.shape
    if c % 128 == 0:
        lhs = jnp.concatenate([framed[b * w : b * w + hw] for b in range(3)], axis=1)
        return jnp.dot(lhs, weights.reshape(9 * c, n), preferred_element_type=F32)
    total = None
    for b in range(3):
        term = jnp.dot(
            framed[b * w : b * w + hw],
            weights[3 * b : 3 * b + 3].reshape(3 * c, n),
            preferred_element_type=F32,
        )
        total = term if total is None else total + term
    return total


def depth_taps(where, weights, rows=None):
    return weights[pl.ds(where * 9, 9)] if rows is None else weights[pl.ds(where * 9, 9), rows]


def per_device(ns, nc, volume, w_first, b_first, w_second, b_second):
    cb, _, h, w = volume.shape
    hw = h * w
    ob = w_first.shape[2]
    full = w_second.shape[2]
    own_out = full // nc
    framed_mid = sds(((h + 2) * w, 3 * ob), BF16)
    volume = volume.reshape(cb, h, w)
    w_first = jnp.transpose(w_first, (1, 0, 2))
    w_second = jnp.transpose(w_second, (1, 0, 2))
    b_first = b_first.reshape(1, ob)
    b_second = b_second.reshape(1, own_out)

    pairs = [(i, i ^ 1) for i in range(ns)]
    beside = [(i, i + 1) for i in range(1, ns - 1, 2)]
    beside = beside + [(j, i) for i, j in beside]
    in_chip = lambda x: lax.ppermute(x, "space", pairs)
    next_chip = lambda x: lax.ppermute(x, "space", beside)
    round_chan = lambda x, k: lax.ppermute(
        x, "chan", [(i, (i + k) % nc) for i in range(nc)]
    )
    across = lambda x, k: lax.ppermute(
        x,
        ("space", "chan"),
        [(i * nc + c, j * nc + (c + k) % nc) for i, j in beside for c in range(nc)],
    )

    def odd():
        return lax.rem(lax.axis_index("space"), 2)

    def chan_rows(k, size):
        owner = lax.rem(lax.axis_index("chan") + nc - k, nc)
        return pl.ds(pl.multiple_of(owner * size, size), size)

    from_pair = lambda: 2 - 2 * odd()
    from_next = lambda: 2 * odd()
    to_next = lambda: 2 - 2 * odd()

    part = sds((hw, ob), F32)
    half = sds((hw, ob), BF16)
    scratch_in = [pltpu.VMEM(((h + 2) * w, 3 * cb), BF16)]
    others = list(range(1, nc))

    arrived = [round_chan(volume, k) for k in others]
    partner = in_chip(volume)
    beyond = next_chip(volume)
    beyond_rest = [across(volume, k) for k in others]
    pieces = 2

    def spread(framed, vol, wt, offsets, k):
        lay_columns(rows_last(vol), framed, h, w)
        taps = [depth_taps(offset(), wt, chan_rows(k, cb)) for offset in offsets]
        if ob % 128 == 0:
            return nine_taps(framed, jnp.concatenate(taps, axis=2), h, w)
        return jnp.concatenate([nine_taps(framed, t, h, w) for t in taps], axis=1)

    def first_own(vol_hbm, wt_hbm, both_ref, wt, framed, vol, sems):
        get_vol = pltpu.make_async_copy(vol_hbm, vol, sems.at[0])
        get_wt = pltpu.make_async_copy(wt_hbm, wt, sems.at[1])
        get_vol.start()
        get_wt.start()
        get_vol.wait()
        get_wt.wait()
        both_ref[...] = spread(framed, vol[...], wt, (lambda: 1, to_next), 0)

    hbm = pl.BlockSpec(memory_space=pltpu.HBM)
    vmem = pl.BlockSpec(memory_space=pltpu.VMEM)
    both, taps_first = pl.pallas_call(
        first_own,
        out_shape=[sds((hw, 2 * ob), F32), sds(w_first.shape, BF16)],
        in_specs=[hbm, hbm],
        out_specs=[vmem, vmem],
        scratch_shapes=[
            *scratch_in,
            pltpu.VMEM(volume.shape, BF16),
            pltpu.SemaphoreType.DMA((2,)),
        ],
        compiler_params=pltpu.CompilerParams(vmem_limit_bytes=VMEM_LIMIT),
        cost_estimate=pl.CostEstimate(
            flops=36 * hw * cb * ob, bytes_accessed=2 * w_first.size, transcendentals=0
        ),
    )(volume, w_first)

    def first_rest(*refs):
        vols, (wt, both_ref, mid_ref, onward_ref, framed) = refs[: nc - 1], refs[nc - 1 :]
        total = both_ref[...]
        for vol, k in zip(vols, others):
            total += spread(framed, vol[...], wt, (lambda: 1, to_next), k)
        mid_ref[...] = total[:, :ob]
        onward_ref[...] = total[:, ob:]

    both, arrived = lax.optimization_barrier((both, arrived))
    partner_rest = [in_chip(q) for x in arrived for q in jnp.split(x, pieces)]
    mid, onward = run(first_rest, [part, part], (*arrived, taps_first, both), scratch_in, 36 * hw * cb * ob)

    def first_pair(*refs):
        whole_ref, refs = refs[0], refs[1:]
        count = (nc - 1) * pieces
        parts_in, (wt, mid_ref, sum_ref, edge_ref, framed) = refs[:count], refs[count:]
        total = mid_ref[...] + spread(framed, whole_ref[...], wt, (from_pair,), 0)
        for k in others:
            vol = jnp.concatenate([r[...] for r in parts_in[(k - 1) * pieces : k * pieces]])
            total += spread(framed, vol, wt, (from_pair,), k)
        sum_ref[...] = total
        edge_ref[...] = total.astype(BF16)

    so_far, edge_sum = run(
        first_pair, [part, half], (partner, *partner_rest, taps_first, mid), scratch_in, 36 * hw * cb * ob
    )
    next_edge = next_chip(edge_sum)

    def first_next(vol, wt, sum_ref, out, framed):
        out[...] = sum_ref[...] + spread(framed, vol[...], wt, (from_next,), 0)

    side = run(first_next, part, (beyond, taps_first, so_far), scratch_in, 18 * hw * cb * ob)

    def hidden_own(*refs):
        vols, (wt, side_ref, b, out, framed) = refs[: nc - 1], refs[nc - 1 :]
        total = side_ref[...]
        for vol, k in zip(vols, others):
            total += spread(framed, vol[...], wt, (from_next,), k)
        out[...] = jnp.maximum(total + b[...], 0.0).astype(BF16)

    hidden = run(hidden_own, half, (*beyond_rest, taps_first, side, b_first), scratch_in, 18 * hw * cb * ob)
    pair_hidden = [in_chip(hidden[: hw // 2]), in_chip(hidden[hw // 2 :])]

    def second_own(cells, wt, out, framed):
        lay_columns(cells[...].astype(F32), framed, h, w)
        out[...] = nine_taps(framed, depth_taps(1, wt), h, w)

    def second_pair(top, bottom, wt, before, out, framed):
        cells = jnp.concatenate([top[...], bottom[...]], axis=0)
        lay_columns(cells.astype(F32), framed, h, w)
        out[...] = before[...] + nine_taps(framed, depth_taps(2 - 2 * odd(), wt), h, w)

    scratch_mid = [pltpu.VMEM(framed_mid.shape, BF16)]
    whole = sds((hw, full), F32)
    second = run(second_own, whole, (hidden, w_second), scratch_mid)
    second = run(second_pair, whole, (*pair_hidden, w_second, second), scratch_mid)

    def wanted(k):
        owner = lax.rem(lax.axis_index("chan") + k, nc)
        return pl.ds(pl.multiple_of(owner * own_out, own_out), own_out)

    def taps_for(wt, where, k):
        if own_out % 128 == 0:
            return wt[pl.ds(where * 9, 9), :, wanted(k)]
        owner = lax.rem(lax.axis_index("chan") + k, nc)
        taps = wt[pl.ds(where * 9, 9)]
        picked = taps[:, :, 0:own_out]
        for i in range(1, nc):
            picked = jnp.where(owner == i, taps[:, :, i * own_out : (i + 1) * own_out], picked)
        return picked

    def columns_for(ref, k):
        if own_out % 128 == 0:
            return ref[:, wanted(k)]
        owner = lax.rem(lax.axis_index("chan") + k, nc)
        cells = ref[...]
        picked = cells[:, 0:own_out]
        for i in range(1, nc):
            picked = jnp.where(owner == i, cells[:, i * own_out : (i + 1) * own_out], picked)
        return picked

    def lay_edge(edge_ref, mine_ref, b, framed):
        place = lax.axis_index("space")
        inside = jnp.logical_and(place > 0, place < ns - 1)
        total = edge_ref[...].astype(F32) + mine_ref[...] + b[...]
        cells = jnp.where(inside, jnp.maximum(total, 0.0), 0.0)
        lay_columns(cells.astype(BF16).astype(F32), framed, h, w)

    def second_send(edge_ref, mine_ref, b, wt, before, *refs):
        outs, framed = refs[:-1], refs[-1]
        lay_edge(edge_ref, mine_ref, b, framed)
        for k in range(1, nc):
            taps = taps_for(wt, 2 * odd(), k)
            sums = columns_for(before, k) + nine_taps(framed, taps, h, w)
            outs[k - 1][...] = channels_first(sums, h, w).astype(BF16)

    sends = run(
        second_send,
        [sds((own_out, h, w), BF16)] * (nc - 1),
        (next_edge, onward, b_first, w_second, second),
        scratch_mid,
        flops=18 * hw * ob * own_out * (nc - 1),
    )
    parts = [round_chan(sends[k - 1], k) for k in range(1, nc)]

    def second_keep(edge_ref, mine_ref, b_mid, wt, before, b, out, framed):
        lay_edge(edge_ref, mine_ref, b_mid, framed)
        taps = taps_for(wt, 2 * odd(), 0)
        sums = columns_for(before, 0) + nine_taps(framed, taps, h, w)
        out[...] = channels_first(sums + b[...], h, w)

    kept = run(
        second_keep,
        sds((own_out, h, w), F32),
        (next_edge, onward, b_first, w_second, second, b_second),
        scratch_mid,
        flops=18 * hw * ob * own_out,
    )

    def finish(kept_ref, *refs):
        total = kept_ref[...]
        for ref in refs[:-1]:
            total += ref[...].astype(F32)
        refs[-1][...] = jnp.maximum(total, 0.0).astype(BF16)

    result = run(finish, sds((own_out, h, w), BF16), (kept, *parts), flops=2 * hw * own_out)
    return result.reshape(own_out, 1, h, w)


def solution(mesh):
    in_specs = (
        P("chan", "space", None, None),
        P(None, None, "chan"),
        P("chan"),
        P("chan", None, None),
        P("chan"),
    )
    return jax.shard_map(
        functools.partial(per_device, mesh.shape["space"], mesh.shape["chan"]),
        mesh=mesh,
        in_specs=in_specs,
        out_specs=P("chan", "space", None, None),
        check_vma=False,
    )
```

```python
import functools

import jax
import jax.numpy as jnp
from jax import lax
from jax.experimental import pallas as pl
from jax.experimental.pallas import tpu as pltpu
from jax.sharding import PartitionSpec as P

F32 = jnp.float32
BF16 = jnp.bfloat16
VMEM_LIMIT = 20 << 20
FRAME_COST = 1 << 30
PAIR_COST = 1 << 28


def sds(shape, dtype):
    return jax.ShapeDtypeStruct(shape, dtype)


def run(kernel, outs, args, scratch=(), flops=0):
    moved = sum(a.size * a.dtype.itemsize for a in args) if flops else 0
    return pl.pallas_call(
        kernel,
        out_shape=outs,
        scratch_shapes=scratch,
        compiler_params=pltpu.CompilerParams(vmem_limit_bytes=VMEM_LIMIT),
        cost_estimate=pl.CostEstimate(
            flops=flops, bytes_accessed=moved, transcendentals=0
        ),
    )(*args)


def rows_last(block):
    c, h, w = block.shape
    planes = jnp.transpose(block, (1, 0, 2))
    return jnp.concatenate([planes[i].T for i in range(h)], axis=0).astype(F32)


def channels_first(cells, h, w):
    planes = jnp.stack([cells[i * w : (i + 1) * w].T for i in range(h)])
    return jnp.transpose(planes, (1, 0, 2))


def lay_columns(cells, framed, h, w):
    c = cells.shape[1]
    hw = h * w
    column = lax.broadcasted_iota(jnp.int32, (hw, 1), 0) % w
    left = jnp.where(column == 0, 0.0, pltpu.roll(cells, 1, 0))
    right = jnp.where(column == w - 1, 0.0, pltpu.roll(cells, hw - 1, 0))
    blank = jnp.zeros((w, 3 * c), BF16)
    framed[0:w] = blank
    framed[w + hw : 2 * w + hw] = blank
    framed[w : w + hw, 0:c] = left.astype(BF16)
    framed[w : w + hw, c : 2 * c] = cells.astype(BF16)
    framed[w : w + hw, 2 * c : 3 * c] = right.astype(BF16)


def nine_taps(framed, weights, h, w):
    hw = h * w
    _, c, n = weights.shape
    if c % 128 == 0:
        lhs = jnp.concatenate([framed[b * w : b * w + hw] for b in range(3)], axis=1)
        return jnp.dot(lhs, weights.reshape(9 * c, n), preferred_element_type=F32)
    total = None
    for b in range(3):
        term = jnp.dot(
            framed[b * w : b * w + hw],
            weights[3 * b : 3 * b + 3].reshape(3 * c, n),
            preferred_element_type=F32,
        )
        total = term if total is None else total + term
    return total


def depth_taps(where, weights, rows=None):
    return weights[pl.ds(where * 9, 9)] if rows is None else weights[pl.ds(where * 9, 9), rows]


def per_device(ns, nc, volume, w_first, b_first, w_second, b_second):
    cb, _, h, w = volume.shape
    hw = h * w
    ob = w_first.shape[2]
    full = w_second.shape[2]
    own_out = full // nc
    framed_mid = sds(((h + 2) * w, 3 * ob), BF16)
    volume = volume.reshape(cb, h, w)
    w_first = jnp.transpose(w_first, (1, 0, 2))
    w_second = jnp.transpose(w_second, (1, 0, 2))
    b_first = b_first.reshape(1, ob)
    b_second = b_second.reshape(1, own_out)

    pairs = [(i, i ^ 1) for i in range(ns)]
    beside = [(i, i + 1) for i in range(1, ns - 1, 2)]
    beside = beside + [(j, i) for i, j in beside]
    in_chip = lambda x: lax.ppermute(x, "space", pairs)
    next_chip = lambda x: lax.ppermute(x, "space", beside)
    round_chan = lambda x, k: lax.ppermute(
        x, "chan", [(i, (i + k) % nc) for i in range(nc)]
    )

    def odd():
        return lax.rem(lax.axis_index("space"), 2)

    def chan_rows(k, size):
        owner = lax.rem(lax.axis_index("chan") + nc - k, nc)
        return pl.ds(pl.multiple_of(owner * size, size), size)

    from_pair = lambda: 2 - 2 * odd()
    from_next = lambda: 2 * odd()
    to_next = lambda: 2 - 2 * odd()

    part = sds((hw, ob), F32)
    half = sds((hw, ob), BF16)
    scratch_in = [pltpu.VMEM(((h + 2) * w, 3 * cb), BF16)]
    others = list(range(1, nc))

    arrived = [round_chan(volume, k) for k in others]
    partner = in_chip(volume)
    beyond = next_chip(volume)

    def frame_own(vol, framed):
        lay_columns(rows_last(vol[...]), framed, h, w)

    framed_in = sds(((h + 2) * w, 3 * cb), BF16)
    framed_own = run(frame_own, framed_in, (volume,), (), FRAME_COST)
    pieces = 1

    def side_by_side(framed, wt, offsets, k):
        taps = [depth_taps(offset(), wt, chan_rows(k, cb)) for offset in offsets]
        if ob % 128 == 0:
            return nine_taps(framed, jnp.concatenate(taps, axis=2), h, w)
        return jnp.concatenate([nine_taps(framed, t, h, w) for t in taps], axis=1)

    def spread(framed, vol, wt, offsets, k):
        lay_columns(rows_last(vol), framed, h, w)
        return side_by_side(framed, wt, offsets, k)

    def first_own(framed, wt, both_ref):
        both_ref[...] = side_by_side(framed, wt, (lambda: 1, to_next), 0)

    both = run(
        first_own, sds((hw, 2 * ob), F32), (framed_own, w_first), (), 36 * hw * cb * ob
    )
    taps_first = w_first

    def pair_own(vol, wt, out, framed):
        out[...] = spread(framed, vol[...], wt, (from_pair,), 0)

    pair_part = run(pair_own, part, (partner, taps_first), scratch_in, 18 * hw * cb * ob)

    def first_rest(*refs):
        vols, refs = refs[: nc - 1], refs[nc - 1 :]
        wt, both_ref, pair_ref, mid_ref, onward_ref, framed = refs
        total = both_ref[...]
        for vol, k in zip(vols, others):
            total += spread(framed, vol[...], wt, (lambda: 1, to_next), k)
        mid_ref[...] = total[:, :ob] + pair_ref[...]
        onward_ref[...] = total[:, ob:]

    both, pair_part, arrived = lax.optimization_barrier((both, pair_part, arrived))
    mid, onward = run(
        first_rest,
        [part, part],
        (*arrived, taps_first, both, pair_part),
        scratch_in,
        36 * hw * cb * ob,
    )
    mid, onto_chan = lax.optimization_barrier((mid, beyond))
    beyond_rest = [round_chan(onto_chan, k) for k in others]
    partner_rest = [in_chip(q) for x in arrived for q in jnp.split(x, pieces)]

    def first_pair(*refs):
        count = (nc - 1) * pieces
        parts_in, (wt, mid_ref, sum_ref, edge_ref, framed) = refs[:count], refs[count:]
        total = mid_ref[...]
        for k in others:
            vol = jnp.concatenate([r[...] for r in parts_in[(k - 1) * pieces : k * pieces]])
            total += spread(framed, vol, wt, (from_pair,), k)
        sum_ref[...] = total
        edge_ref[...] = total.astype(BF16)

    so_far, edge_sum = run(
        first_pair, [part, half], (*partner_rest, taps_first, mid), scratch_in, PAIR_COST
    )
    next_edge = next_chip(edge_sum)

    def first_next(vol, wt, sum_ref, out, framed):
        out[...] = sum_ref[...] + spread(framed, vol[...], wt, (from_next,), 0)

    side = run(first_next, part, (beyond, taps_first, so_far), scratch_in)

    def hidden_own(*refs):
        vols, (wt, side_ref, b, out, framed) = refs[: nc - 1], refs[nc - 1 :]
        total = side_ref[...]
        for vol, k in zip(vols, others):
            total += spread(framed, vol[...], wt, (from_next,), k)
        out[...] = jnp.maximum(total + b[...], 0.0).astype(BF16)

    hidden = run(hidden_own, half, (*beyond_rest, taps_first, side, b_first), scratch_in)
    pair_hidden = [in_chip(hidden[: hw // 2]), in_chip(hidden[hw // 2 :])]

    def second_own(cells, wt, out, framed):
        lay_columns(cells[...].astype(F32), framed, h, w)
        out[...] = nine_taps(framed, depth_taps(1, wt), h, w)

    scratch_mid = [pltpu.VMEM(framed_mid.shape, BF16)]
    whole = sds((hw, full), F32)
    second = run(second_own, whole, (hidden, w_second), scratch_mid)
    def wanted(k):
        owner = lax.rem(lax.axis_index("chan") + k, nc)
        return pl.ds(pl.multiple_of(owner * own_out, own_out), own_out)

    def taps_for(wt, where, k):
        if own_out % 128 == 0:
            return wt[pl.ds(where * 9, 9), :, wanted(k)]
        owner = lax.rem(lax.axis_index("chan") + k, nc)
        taps = wt[pl.ds(where * 9, 9)]
        picked = taps[:, :, 0:own_out]
        for i in range(1, nc):
            picked = jnp.where(owner == i, taps[:, :, i * own_out : (i + 1) * own_out], picked)
        return picked

    def columns_for(ref, k):
        if own_out % 128 == 0:
            return ref[:, wanted(k)]
        owner = lax.rem(lax.axis_index("chan") + k, nc)
        cells = ref[...]
        picked = cells[:, 0:own_out]
        for i in range(1, nc):
            picked = jnp.where(owner == i, cells[:, i * own_out : (i + 1) * own_out], picked)
        return picked

    def beside(top, low, edge, mine, b, wt, before, frames, ks):
        place = lax.axis_index("space")
        inside = jnp.logical_and(place > 0, place < ns - 1)
        total = edge[...].astype(F32) + mine[...] + b[...]
        edge_cells = jnp.where(inside, jnp.maximum(total, 0.0), 0.0)
        pair_cells = jnp.concatenate([top[...], low[...]], axis=0).astype(F32)
        lay_columns(pair_cells, frames.at[0], h, w)
        lay_columns(edge_cells, frames.at[1], h, w)
        for k in ks:
            sums = nine_taps(frames.at[0], taps_for(wt, 2 - 2 * odd(), k), h, w)
            sums += nine_taps(frames.at[1], taps_for(wt, 2 * odd(), k), h, w)
            yield sums + columns_for(before, k)

    def second_send(*refs):
        ins, outs, frames = refs[:7], refs[7:-1], refs[-1]
        for out, sums in zip(outs, beside(*ins, frames, others)):
            out[...] = sums.astype(BF16)

    def second_keep(*refs):
        ins, (b, out, frames) = refs[:7], refs[7:]
        for sums in beside(*ins, frames, [0]):
            out[...] = sums + b[...]

    two_frames = [pltpu.VMEM((2, (h + 2) * w, 3 * ob), BF16)]
    beside_in = (*pair_hidden, next_edge, onward, b_first, w_second, second)
    sends = run(second_send, [sds((hw, own_out), BF16)] * (nc - 1), beside_in, two_frames)
    parts = [round_chan(sends[k - 1], k) for k in others]
    kept = run(
        second_keep,
        sds((hw, own_out), F32),
        (*beside_in, b_second),
        two_frames,
        flops=36 * hw * ob * own_out,
    )

    def finish(kept_ref, *refs):
        total, out = kept_ref[...], refs[-1]
        for ref in refs[:-1]:
            total += ref[...].astype(F32)
        out[...] = channels_first(jnp.maximum(total, 0.0), h, w).astype(BF16)

    result = run(finish, sds((own_out, h, w), BF16), (kept, *parts), flops=2 * hw * own_out)
    return result.reshape(own_out, 1, h, w)


def solution(mesh):
    in_specs = (
        P("chan", "space", None, None),
        P(None, None, "chan"),
        P("chan"),
        P("chan", None, None),
        P("chan"),
    )
    return jax.shard_map(
        functools.partial(per_device, mesh.shape["space"], mesh.shape["chan"]),
        mesh=mesh,
        in_specs=in_specs,
        out_specs=P("chan", "space", None, None),
        check_vma=False,
    )
```

```python
import functools

import jax
import jax.numpy as jnp
from jax import lax
from jax.experimental import pallas as pl
from jax.experimental.pallas import tpu as pltpu
from jax.sharding import PartitionSpec as P

F32 = jnp.float32
BF16 = jnp.bfloat16
VMEM_LIMIT = 20 << 20
FRAME_COST = 1 << 30
PAIR_COST = 1 << 28


def sds(shape, dtype):
    return jax.ShapeDtypeStruct(shape, dtype)


def run(kernel, outs, args, scratch=(), flops=0):
    moved = sum(a.size * a.dtype.itemsize for a in args) if flops else 0
    return pl.pallas_call(
        kernel,
        out_shape=outs,
        scratch_shapes=scratch,
        compiler_params=pltpu.CompilerParams(vmem_limit_bytes=VMEM_LIMIT),
        cost_estimate=pl.CostEstimate(
            flops=flops, bytes_accessed=moved, transcendentals=0
        ),
    )(*args)


def rows_last(block):
    c, h, w = block.shape
    planes = jnp.transpose(block, (1, 0, 2))
    return jnp.concatenate([planes[i].T for i in range(h)], axis=0).astype(F32)


def channels_first(cells, h, w):
    planes = jnp.stack([cells[i * w : (i + 1) * w].T for i in range(h)])
    return jnp.transpose(planes, (1, 0, 2))


def lay_columns(cells, framed, h, w):
    c = cells.shape[1]
    hw = h * w
    column = lax.broadcasted_iota(jnp.int32, (hw, 1), 0) % w
    left = jnp.where(column == 0, 0.0, pltpu.roll(cells, 1, 0))
    right = jnp.where(column == w - 1, 0.0, pltpu.roll(cells, hw - 1, 0))
    blank = jnp.zeros((w, 3 * c), BF16)
    framed[0:w] = blank
    framed[w + hw : 2 * w + hw] = blank
    framed[w : w + hw, 0:c] = left.astype(BF16)
    framed[w : w + hw, c : 2 * c] = cells.astype(BF16)
    framed[w : w + hw, 2 * c : 3 * c] = right.astype(BF16)


def nine_taps(framed, weights, h, w):
    hw = h * w
    _, c, n = weights.shape
    if c % 128 == 0:
        lhs = jnp.concatenate([framed[b * w : b * w + hw] for b in range(3)], axis=1)
        return jnp.dot(lhs, weights.reshape(9 * c, n), preferred_element_type=F32)
    total = None
    for b in range(3):
        term = jnp.dot(
            framed[b * w : b * w + hw],
            weights[3 * b : 3 * b + 3].reshape(3 * c, n),
            preferred_element_type=F32,
        )
        total = term if total is None else total + term
    return total


def depth_taps(where, weights, rows=None):
    return weights[pl.ds(where * 9, 9)] if rows is None else weights[pl.ds(where * 9, 9), rows]


def per_device(ns, nc, volume, w_first, b_first, w_second, b_second):
    cb, _, h, w = volume.shape
    hw = h * w
    ob = w_first.shape[2]
    full = w_second.shape[2]
    own_out = full // nc
    framed_mid = sds(((h + 2) * w, 3 * ob), BF16)
    volume = volume.reshape(cb, h, w)
    w_first = jnp.transpose(w_first, (1, 0, 2))
    w_second = jnp.transpose(w_second, (1, 0, 2))
    b_first = b_first.reshape(1, ob)
    b_second = b_second.reshape(1, own_out)

    pairs = [(i, i ^ 1) for i in range(ns)]
    beside = [(i, i + 1) for i in range(1, ns - 1, 2)]
    beside = beside + [(j, i) for i, j in beside]
    in_chip = lambda x: lax.ppermute(x, "space", pairs)
    next_chip = lambda x: lax.ppermute(x, "space", beside)
    round_chan = lambda x, k: lax.ppermute(
        x, "chan", [(i, (i + k) % nc) for i in range(nc)]
    )

    def odd():
        return lax.rem(lax.axis_index("space"), 2)

    def chan_rows(k, size):
        owner = lax.rem(lax.axis_index("chan") + nc - k, nc)
        return pl.ds(pl.multiple_of(owner * size, size), size)

    from_pair = lambda: 2 - 2 * odd()
    from_next = lambda: 2 * odd()
    to_next = lambda: 2 - 2 * odd()

    part = sds((hw, ob), F32)
    half = sds((hw, ob), BF16)
    scratch_in = [pltpu.VMEM(((h + 2) * w, 3 * cb), BF16)]
    others = list(range(1, nc))

    arrived = [round_chan(volume, k) for k in others]
    partner = in_chip(volume)
    beyond = next_chip(volume)

    def frame_own(vol, framed):
        lay_columns(rows_last(vol[...]), framed, h, w)

    framed_in = sds(((h + 2) * w, 3 * cb), BF16)
    framed_own = run(frame_own, framed_in, (volume,), (), FRAME_COST)
    pieces = 1

    def side_by_side(framed, wt, offsets, k):
        taps = [depth_taps(offset(), wt, chan_rows(k, cb)) for offset in offsets]
        if ob % 128 == 0:
            return nine_taps(framed, jnp.concatenate(taps, axis=2), h, w)
        return jnp.concatenate([nine_taps(framed, t, h, w) for t in taps], axis=1)

    def spread(framed, vol, wt, offsets, k):
        lay_columns(rows_last(vol), framed, h, w)
        return side_by_side(framed, wt, offsets, k)

    def first_own(framed, wt, both_ref):
        both_ref[...] = side_by_side(framed, wt, (lambda: 1, to_next), 0)

    both = run(
        first_own, sds((hw, 2 * ob), F32), (framed_own, w_first), (), 36 * hw * cb * ob
    )
    taps_first = w_first

    def first_rest(*refs):
        vols, refs = refs[: nc - 1], refs[nc - 1 :]
        wt, both_ref, mid_ref, onward_ref, framed = refs
        total = both_ref[...]
        for vol, k in zip(vols, others):
            total += spread(framed, vol[...], wt, (lambda: 1, to_next), k)
        mid_ref[...] = total[:, :ob]
        onward_ref[...] = total[:, ob:]

    both, arrived = lax.optimization_barrier((both, arrived))
    mid, onward = run(
        first_rest,
        [part, part],
        (*arrived, taps_first, both),
        scratch_in,
        36 * hw * cb * ob,
    )
    mid, onto_chan = lax.optimization_barrier((mid, beyond))
    beyond_rest = [round_chan(onto_chan, k) for k in others]
    partner_rest = [in_chip(q) for x in arrived for q in jnp.split(x, pieces)]

    def first_pair(*refs):
        whole_ref, refs = refs[0], refs[1:]
        count = (nc - 1) * pieces
        parts_in, (wt, mid_ref, sum_ref, edge_ref, framed) = refs[:count], refs[count:]
        total = mid_ref[...] + spread(framed, whole_ref[...], wt, (from_pair,), 0)
        for k in others:
            vol = jnp.concatenate([r[...] for r in parts_in[(k - 1) * pieces : k * pieces]])
            total += spread(framed, vol, wt, (from_pair,), k)
        sum_ref[...] = total
        edge_ref[...] = total.astype(BF16)

    so_far, edge_sum = run(
        first_pair, [part, half], (partner, *partner_rest, taps_first, mid), scratch_in, PAIR_COST
    )
    next_edge = next_chip(edge_sum)

    def first_next(vol, wt, sum_ref, out, framed):
        out[...] = sum_ref[...] + spread(framed, vol[...], wt, (from_next,), 0)

    side = run(first_next, part, (beyond, taps_first, so_far), scratch_in)

    def hidden_own(*refs):
        vols, (wt, side_ref, b, out, framed) = refs[: nc - 1], refs[nc - 1 :]
        total = side_ref[...]
        for vol, k in zip(vols, others):
            total += spread(framed, vol[...], wt, (from_next,), k)
        out[...] = jnp.maximum(total + b[...], 0.0).astype(BF16)

    hidden = run(hidden_own, half, (*beyond_rest, taps_first, side, b_first), scratch_in)
    pair_hidden = [in_chip(hidden[: hw // 2]), in_chip(hidden[hw // 2 :])]

    def second_own(cells, wt, out, framed):
        lay_columns(cells[...].astype(F32), framed, h, w)
        out[...] = nine_taps(framed, depth_taps(1, wt), h, w)

    scratch_mid = [pltpu.VMEM(framed_mid.shape, BF16)]
    whole = sds((hw, full), F32)
    second = run(second_own, whole, (hidden, w_second), scratch_mid)
    def wanted(k):
        owner = lax.rem(lax.axis_index("chan") + k, nc)
        return pl.ds(pl.multiple_of(owner * own_out, own_out), own_out)

    def taps_for(wt, where, k):
        if own_out % 128 == 0:
            return wt[pl.ds(where * 9, 9), :, wanted(k)]
        owner = lax.rem(lax.axis_index("chan") + k, nc)
        taps = wt[pl.ds(where * 9, 9)]
        picked = taps[:, :, 0:own_out]
        for i in range(1, nc):
            picked = jnp.where(owner == i, taps[:, :, i * own_out : (i + 1) * own_out], picked)
        return picked

    def columns_for(ref, k):
        if own_out % 128 == 0:
            return ref[:, wanted(k)]
        owner = lax.rem(lax.axis_index("chan") + k, nc)
        cells = ref[...]
        picked = cells[:, 0:own_out]
        for i in range(1, nc):
            picked = jnp.where(owner == i, cells[:, i * own_out : (i + 1) * own_out], picked)
        return picked

    def beside(top, low, edge, mine, b, wt, before, frames, ks):
        place = lax.axis_index("space")
        inside = jnp.logical_and(place > 0, place < ns - 1)
        total = edge[...].astype(F32) + mine[...] + b[...]
        edge_cells = jnp.where(inside, jnp.maximum(total, 0.0), 0.0)
        pair_cells = jnp.concatenate([top[...], low[...]], axis=0).astype(F32)
        lay_columns(pair_cells, frames.at[0], h, w)
        lay_columns(edge_cells, frames.at[1], h, w)
        for k in ks:
            sums = nine_taps(frames.at[0], taps_for(wt, 2 - 2 * odd(), k), h, w)
            sums += nine_taps(frames.at[1], taps_for(wt, 2 * odd(), k), h, w)
            yield sums + columns_for(before, k)

    def second_send(*refs):
        ins, outs, frames = refs[:7], refs[7:-1], refs[-1]
        for out, sums in zip(outs, beside(*ins, frames, others)):
            out[...] = sums.astype(BF16)

    def second_keep(*refs):
        ins, (b, out, frames) = refs[:7], refs[7:]
        for sums in beside(*ins, frames, [0]):
            out[...] = sums + b[...]

    two_frames = [pltpu.VMEM((2, (h + 2) * w, 3 * ob), BF16)]
    beside_in = (*pair_hidden, next_edge, onward, b_first, w_second, second)
    sends = run(second_send, [sds((hw, own_out), BF16)] * (nc - 1), beside_in, two_frames)
    parts = [round_chan(sends[k - 1], k) for k in others]
    kept = run(
        second_keep,
        sds((hw, own_out), F32),
        (*beside_in, b_second),
        two_frames,
        flops=36 * hw * ob * own_out,
    )

    def finish(kept_ref, *refs):
        total, out = kept_ref[...], refs[-1]
        for ref in refs[:-1]:
            total += ref[...].astype(F32)
        out[...] = channels_first(jnp.maximum(total, 0.0), h, w).astype(BF16)

    result = run(finish, sds((own_out, h, w), BF16), (kept, *parts), flops=2 * hw * own_out)
    return result.reshape(own_out, 1, h, w)


def solution(mesh):
    in_specs = (
        P("chan", "space", None, None),
        P(None, None, "chan"),
        P("chan"),
        P("chan", None, None),
        P("chan"),
    )
    return jax.shard_map(
        functools.partial(per_device, mesh.shape["space"], mesh.shape["chan"]),
        mesh=mesh,
        in_specs=in_specs,
        out_specs=P("chan", "space", None, None),
        check_vma=False,
    )
```

```python
import functools

import jax
import jax.numpy as jnp
from jax import lax
from jax.experimental import pallas as pl
from jax.experimental.pallas import tpu as pltpu
from jax.sharding import PartitionSpec as P

F32 = jnp.float32
BF16 = jnp.bfloat16
VMEM_LIMIT = 20 << 20
FRAME_COST = 1 << 30
PAIR_COST = 1 << 28


def sds(shape, dtype):
    return jax.ShapeDtypeStruct(shape, dtype)


def run(kernel, outs, args, scratch=(), flops=0):
    moved = sum(a.size * a.dtype.itemsize for a in args) if flops else 0
    return pl.pallas_call(
        kernel,
        out_shape=outs,
        scratch_shapes=scratch,
        compiler_params=pltpu.CompilerParams(vmem_limit_bytes=VMEM_LIMIT),
        cost_estimate=pl.CostEstimate(
            flops=flops, bytes_accessed=moved, transcendentals=0
        ),
    )(*args)


def rows_last(block):
    c, h, w = block.shape
    planes = jnp.transpose(block, (1, 0, 2))
    return jnp.concatenate([planes[i].T for i in range(h)], axis=0).astype(F32)


def channels_first(cells, h, w):
    planes = jnp.stack([cells[i * w : (i + 1) * w].T for i in range(h)])
    return jnp.transpose(planes, (1, 0, 2))


def lay_columns(cells, framed, h, w):
    c = cells.shape[1]
    hw = h * w
    column = lax.broadcasted_iota(jnp.int32, (hw, 1), 0) % w
    left = jnp.where(column == 0, 0.0, pltpu.roll(cells, 1, 0))
    right = jnp.where(column == w - 1, 0.0, pltpu.roll(cells, hw - 1, 0))
    blank = jnp.zeros((w, 3 * c), BF16)
    framed[0:w] = blank
    framed[w + hw : 2 * w + hw] = blank
    framed[w : w + hw, 0:c] = left.astype(BF16)
    framed[w : w + hw, c : 2 * c] = cells.astype(BF16)
    framed[w : w + hw, 2 * c : 3 * c] = right.astype(BF16)


def nine_taps(framed, weights, h, w, first=0):
    hw = h * w
    _, c, n = weights.shape
    at = [slice((first + b) * w, (first + b) * w + hw) for b in range(3)]
    if c % 128 == 0:
        lhs = jnp.concatenate([framed[rows] for rows in at], axis=1)
        return jnp.dot(lhs, weights.reshape(9 * c, n), preferred_element_type=F32)
    total = None
    for b in range(3):
        term = jnp.dot(
            framed[at[b]],
            weights[3 * b : 3 * b + 3].reshape(3 * c, n),
            preferred_element_type=F32,
        )
        total = term if total is None else total + term
    return total


def depth_taps(where, weights, rows=None):
    return weights[pl.ds(where * 9, 9)] if rows is None else weights[pl.ds(where * 9, 9), rows]


def per_device(ns, nc, volume, w_first, b_first, w_second, b_second):
    cb, _, h, w = volume.shape
    hw = h * w
    ob = w_first.shape[2]
    full = w_second.shape[2]
    own_out = full // nc
    framed_mid = sds(((h + 2) * w, 3 * ob), BF16)
    volume = volume.reshape(cb, h, w)
    w_first = jnp.transpose(w_first, (1, 0, 2))
    w_second = jnp.transpose(w_second, (1, 0, 2))
    b_first = b_first.reshape(1, ob)
    b_second = b_second.reshape(1, own_out)

    pairs = [(i, i ^ 1) for i in range(ns)]
    beside = [(i, i + 1) for i in range(1, ns - 1, 2)]
    beside = beside + [(j, i) for i, j in beside]
    in_chip = lambda x: lax.ppermute(x, "space", pairs)
    next_chip = lambda x: lax.ppermute(x, "space", beside)
    round_chan = lambda x, k: lax.ppermute(
        x, "chan", [(i, (i + k) % nc) for i in range(nc)]
    )

    def odd():
        return lax.rem(lax.axis_index("space"), 2)

    def chan_rows(k, size):
        owner = lax.rem(lax.axis_index("chan") + nc - k, nc)
        return pl.ds(pl.multiple_of(owner * size, size), size)

    from_pair = lambda: 2 - 2 * odd()
    from_next = lambda: 2 * odd()
    to_next = lambda: 2 - 2 * odd()

    part = sds((hw, ob), F32)
    half = sds((hw, ob), BF16)
    scratch_in = [pltpu.VMEM(((h + 2) * w, 3 * cb), BF16)]
    others = list(range(1, nc))

    arrived = [round_chan(volume, k) for k in others]
    partner = in_chip(volume)
    beyond = next_chip(volume)

    def frame_own(vol, framed):
        lay_columns(rows_last(vol[...]), framed, h, w)

    framed_in = sds(((h + 2) * w, 3 * cb), BF16)
    framed_own = run(frame_own, framed_in, (volume,), (), FRAME_COST)
    pieces = 1

    def side_by_side(framed, wt, offsets, k):
        taps = [depth_taps(offset(), wt, chan_rows(k, cb)) for offset in offsets]
        if ob % 128 == 0:
            return nine_taps(framed, jnp.concatenate(taps, axis=2), h, w)
        return jnp.concatenate([nine_taps(framed, t, h, w) for t in taps], axis=1)

    def spread(framed, vol, wt, offsets, k):
        lay_columns(rows_last(vol), framed, h, w)
        return side_by_side(framed, wt, offsets, k)

    def first_own(framed, wt, both_ref):
        both_ref[...] = side_by_side(framed, wt, (lambda: 1, to_next), 0)

    both = run(
        first_own, sds((hw, 2 * ob), F32), (framed_own, w_first), (), 36 * hw * cb * ob
    )
    taps_first = w_first

    def first_rest(*refs):
        vols, refs = refs[: nc - 1], refs[nc - 1 :]
        wt, both_ref, mid_ref, onward_ref, framed = refs
        total = both_ref[...]
        for vol, k in zip(vols, others):
            total += spread(framed, vol[...], wt, (lambda: 1, to_next), k)
        mid_ref[...] = total[:, :ob]
        onward_ref[...] = total[:, ob:]

    both, arrived = lax.optimization_barrier((both, arrived))
    mid, onward = run(
        first_rest,
        [part, part],
        (*arrived, taps_first, both),
        scratch_in,
        36 * hw * cb * ob,
    )
    mid, onto_chan = lax.optimization_barrier((mid, beyond))
    beyond_rest = [round_chan(onto_chan, k) for k in others]
    partner_rest = [in_chip(q) for x in arrived for q in jnp.split(x, pieces)]

    def first_pair(*refs):
        whole_ref, refs = refs[0], refs[1:]
        count = (nc - 1) * pieces
        parts_in, (wt, mid_ref, sum_ref, edge_ref, framed) = refs[:count], refs[count:]
        total = mid_ref[...] + spread(framed, whole_ref[...], wt, (from_pair,), 0)
        for k in others:
            vol = jnp.concatenate([r[...] for r in parts_in[(k - 1) * pieces : k * pieces]])
            total += spread(framed, vol, wt, (from_pair,), k)
        sum_ref[...] = total
        edge_ref[...] = total.astype(BF16)

    so_far, edge_sum = run(
        first_pair, [part, half], (partner, *partner_rest, taps_first, mid), scratch_in, PAIR_COST
    )
    next_edge = next_chip(edge_sum)

    def first_next(vol, wt, sum_ref, out, framed):
        out[...] = sum_ref[...] + spread(framed, vol[...], wt, (from_next,), 0)

    side = run(first_next, part, (beyond, taps_first, so_far), scratch_in)

    def hidden_own(*refs):
        vols, (wt, side_ref, b, out, framed) = refs[: nc - 1], refs[nc - 1 :]
        total = side_ref[...]
        for vol, k in zip(vols, others):
            total += spread(framed, vol[...], wt, (from_next,), k)
        out[...] = jnp.maximum(total + b[...], 0.0).astype(BF16)

    hidden = run(hidden_own, half, (*beyond_rest, taps_first, side, b_first), scratch_in)
    pair_hidden = [in_chip(hidden[: hw // 2]), in_chip(hidden[hw // 2 :])]

    def second_own(cells, wt, out, framed):
        lay_columns(cells[...].astype(F32), framed, h, w)
        out[...] = nine_taps(framed, depth_taps(1, wt), h, w)

    scratch_mid = [pltpu.VMEM(framed_mid.shape, BF16)]
    whole = sds((hw, full), F32)
    second = run(second_own, whole, (hidden, w_second), scratch_mid)
    def wanted(k):
        owner = lax.rem(lax.axis_index("chan") + k, nc)
        return pl.ds(pl.multiple_of(owner * own_out, own_out), own_out)

    def taps_for(wt, where, k):
        if own_out % 128 == 0:
            return wt[pl.ds(where * 9, 9), :, wanted(k)]
        owner = lax.rem(lax.axis_index("chan") + k, nc)
        taps = wt[pl.ds(where * 9, 9)]
        picked = taps[:, :, 0:own_out]
        for i in range(1, nc):
            picked = jnp.where(owner == i, taps[:, :, i * own_out : (i + 1) * own_out], picked)
        return picked

    def columns_for(ref, rows, k):
        if own_out % 128 == 0:
            return ref[rows, wanted(k)]
        owner = lax.rem(lax.axis_index("chan") + k, nc)
        cells = ref[rows]
        picked = cells[:, 0:own_out]
        for i in range(1, nc):
            picked = jnp.where(owner == i, cells[:, i * own_out : (i + 1) * own_out], picked)
        return picked

    def beside_rows(top, low, edge, mine, b, wt, before, frames, ks, start, stop):
        first, last = max(start - 1, 0), min(stop + 1, h)
        rows = slice(first * w, last * w)
        count = last - first
        pair_cells = jnp.concatenate([top[...], low[...]], axis=0)[rows].astype(F32)
        place = lax.axis_index("space")
        inside = jnp.logical_and(place > 0, place < ns - 1)
        total = edge[rows].astype(F32) + mine[rows] + b[...]
        edge_cells = jnp.where(inside, jnp.maximum(total, 0.0), 0.0)
        lay_columns(pair_cells, frames.at[0], count, w)
        lay_columns(edge_cells, frames.at[1], count, w)
        skip = start - first
        out = []
        for k in ks:
            sums = columns_for(before, slice(start * w, stop * w), k)
            taps = taps_for(wt, 2 - 2 * odd(), k)
            sums += nine_taps(frames.at[0], taps, stop - start, w, skip)
            taps = taps_for(wt, 2 * odd(), k)
            sums += nine_taps(frames.at[1], taps, stop - start, w, skip)
            out.append(sums)
        return out

    def send_rows(start, stop):
        def kernel(*refs):
            ins, outs, frames = refs[:7], refs[7:-1], refs[-1]
            for out, sums in zip(outs, beside_rows(*ins, frames, others, start, stop)):
                out[...] = sums.astype(BF16)

        return kernel

    two_frames = [pltpu.VMEM((2, (h + 2) * w, 3 * ob), BF16)]
    beside_in = (*pair_hidden, next_edge, onward, b_first, w_second, second)
    chunks = [(0, h // 2), (h // 2, h)]
    parts = []
    for start, stop in chunks:
        sends = run(
            send_rows(start, stop),
            [sds(((stop - start) * w, own_out), BF16)] * (nc - 1),
            beside_in,
            two_frames,
        )
        parts.append([round_chan(sends[k - 1], k) for k in others])

    def second_keep(*refs):
        ins, (b, out, frames) = refs[:7], refs[7:]
        out[...] = beside_rows(*ins, frames, [0], 0, h)[0] + b[...]

    kept = run(
        second_keep,
        sds((hw, own_out), F32),
        (*beside_in, b_second),
        two_frames,
        flops=36 * hw * ob * own_out,
    )

    def finish(kept_ref, *refs):
        total, out = kept_ref[...], refs[-1]
        for k in range(nc - 1):
            pieces_in = [refs[i * (nc - 1) + k][...] for i in range(len(chunks))]
            total += jnp.concatenate(pieces_in, axis=0).astype(F32)
        out[...] = channels_first(jnp.maximum(total, 0.0), h, w).astype(BF16)

    result = run(
        finish,
        sds((own_out, h, w), BF16),
        (kept, *[x for part in parts for x in part]),
        flops=2 * hw * own_out,
    )
    return result.reshape(own_out, 1, h, w)


def solution(mesh):
    in_specs = (
        P("chan", "space", None, None),
        P(None, None, "chan"),
        P("chan"),
        P("chan", None, None),
        P("chan"),
    )
    return jax.shard_map(
        functools.partial(per_device, mesh.shape["space"], mesh.shape["chan"]),
        mesh=mesh,
        in_specs=in_specs,
        out_specs=P("chan", "space", None, None),
        check_vma=False,
    )
```

```python
import functools

import jax
import jax.numpy as jnp
from jax import lax
from jax.experimental import pallas as pl
from jax.experimental.pallas import tpu as pltpu
from jax.sharding import PartitionSpec as P

F32 = jnp.float32
BF16 = jnp.bfloat16
VMEM_LIMIT = 20 << 20
FRAME_COST = 1 << 30
PAIR_COST = 1 << 28


def sds(shape, dtype):
    return jax.ShapeDtypeStruct(shape, dtype)


def run(kernel, outs, args, scratch=(), flops=0):
    moved = sum(a.size * a.dtype.itemsize for a in args) if flops else 0
    return pl.pallas_call(
        kernel,
        out_shape=outs,
        scratch_shapes=scratch,
        compiler_params=pltpu.CompilerParams(vmem_limit_bytes=VMEM_LIMIT),
        cost_estimate=pl.CostEstimate(
            flops=flops, bytes_accessed=moved, transcendentals=0
        ),
    )(*args)


def rows_last(block):
    c, h, w = block.shape
    planes = jnp.transpose(block, (1, 0, 2))
    return jnp.concatenate([planes[i].T for i in range(h)], axis=0).astype(F32)


def channels_first(cells, h, w):
    planes = jnp.stack([cells[i * w : (i + 1) * w].T for i in range(h)])
    return jnp.transpose(planes, (1, 0, 2))


def lay_columns(cells, framed, h, w):
    c = cells.shape[1]
    hw = h * w
    column = lax.broadcasted_iota(jnp.int32, (hw, 1), 0) % w
    left = jnp.where(column == 0, 0.0, pltpu.roll(cells, 1, 0))
    right = jnp.where(column == w - 1, 0.0, pltpu.roll(cells, hw - 1, 0))
    blank = jnp.zeros((w, 3 * c), BF16)
    framed[0:w] = blank
    framed[w + hw : 2 * w + hw] = blank
    framed[w : w + hw, 0:c] = left.astype(BF16)
    framed[w : w + hw, c : 2 * c] = cells.astype(BF16)
    framed[w : w + hw, 2 * c : 3 * c] = right.astype(BF16)


def nine_taps(framed, weights, h, w, first=0):
    hw = h * w
    _, c, n = weights.shape
    at = [slice((first + b) * w, (first + b) * w + hw) for b in range(3)]
    if c % 128 == 0:
        lhs = jnp.concatenate([framed[rows] for rows in at], axis=1)
        return jnp.dot(lhs, weights.reshape(9 * c, n), preferred_element_type=F32)
    total = None
    for b in range(3):
        term = jnp.dot(
            framed[at[b]],
            weights[3 * b : 3 * b + 3].reshape(3 * c, n),
            preferred_element_type=F32,
        )
        total = term if total is None else total + term
    return total


def depth_taps(where, weights, rows=None):
    return weights[pl.ds(where * 9, 9)] if rows is None else weights[pl.ds(where * 9, 9), rows]


def per_device(ns, nc, volume, w_first, b_first, w_second, b_second):
    cb, _, h, w = volume.shape
    hw = h * w
    ob = w_first.shape[2]
    full = w_second.shape[2]
    own_out = full // nc
    framed_mid = sds(((h + 2) * w, 3 * ob), BF16)
    volume = volume.reshape(cb, h, w)
    w_first = jnp.transpose(w_first, (1, 0, 2))
    w_second = jnp.transpose(w_second, (1, 0, 2))
    b_first = b_first.reshape(1, ob)
    b_second = b_second.reshape(1, own_out)

    pairs = [(i, i ^ 1) for i in range(ns)]
    beside = [(i, i + 1) for i in range(1, ns - 1, 2)]
    beside = beside + [(j, i) for i, j in beside]
    in_chip = lambda x: lax.ppermute(x, "space", pairs)
    next_chip = lambda x: lax.ppermute(x, "space", beside)
    round_chan = lambda x, k: lax.ppermute(
        x, "chan", [(i, (i + k) % nc) for i in range(nc)]
    )

    def odd():
        return lax.rem(lax.axis_index("space"), 2)

    def chan_rows(k, size):
        owner = lax.rem(lax.axis_index("chan") + nc - k, nc)
        return pl.ds(pl.multiple_of(owner * size, size), size)

    from_pair = lambda: 2 - 2 * odd()
    from_next = lambda: 2 * odd()
    to_next = lambda: 2 - 2 * odd()

    part = sds((hw, ob), F32)
    half = sds((hw, ob), BF16)
    scratch_in = [pltpu.VMEM(((h + 2) * w, 3 * cb), BF16)]
    others = list(range(1, nc))

    arrived = [round_chan(volume, k) for k in others]
    partner = in_chip(volume)
    beyond = next_chip(volume)

    def frame_own(vol, framed):
        lay_columns(rows_last(vol[...]), framed, h, w)

    framed_in = sds(((h + 2) * w, 3 * cb), BF16)
    framed_own = run(frame_own, framed_in, (volume,), (), FRAME_COST)
    pieces = 1

    def side_by_side(framed, wt, offsets, k):
        taps = [depth_taps(offset(), wt, chan_rows(k, cb)) for offset in offsets]
        if ob % 128 == 0:
            return nine_taps(framed, jnp.concatenate(taps, axis=2), h, w)
        return jnp.concatenate([nine_taps(framed, t, h, w) for t in taps], axis=1)

    def spread(framed, vol, wt, offsets, k):
        lay_columns(rows_last(vol), framed, h, w)
        return side_by_side(framed, wt, offsets, k)

    def first_own(framed, wt, both_ref):
        both_ref[...] = side_by_side(framed, wt, (lambda: 1, to_next), 0)

    both = run(
        first_own, sds((hw, 2 * ob), F32), (framed_own, w_first), (), 36 * hw * cb * ob
    )
    taps_first = w_first

    def first_rest(*refs):
        vols, refs = refs[: nc - 1], refs[nc - 1 :]
        wt, both_ref, mid_ref, onward_ref, framed = refs
        total = both_ref[...]
        for vol, k in zip(vols, others):
            total += spread(framed, vol[...], wt, (lambda: 1, to_next), k)
        mid_ref[...] = total[:, :ob]
        onward_ref[...] = total[:, ob:]

    both, arrived = lax.optimization_barrier((both, arrived))
    mid, onward = run(
        first_rest,
        [part, part],
        (*arrived, taps_first, both),
        scratch_in,
        36 * hw * cb * ob,
    )
    mid, onto_chan = lax.optimization_barrier((mid, beyond))
    beyond_rest = [round_chan(onto_chan, k) for k in others]
    partner_rest = [in_chip(q) for x in arrived for q in jnp.split(x, pieces)]

    def first_pair(*refs):
        whole_ref, refs = refs[0], refs[1:]
        count = (nc - 1) * pieces
        parts_in, (wt, mid_ref, sum_ref, edge_ref, framed) = refs[:count], refs[count:]
        total = mid_ref[...] + spread(framed, whole_ref[...], wt, (from_pair,), 0)
        for k in others:
            vol = jnp.concatenate([r[...] for r in parts_in[(k - 1) * pieces : k * pieces]])
            total += spread(framed, vol, wt, (from_pair,), k)
        sum_ref[...] = total
        edge_ref[...] = total.astype(BF16)

    so_far, edge_sum = run(
        first_pair, [part, half], (partner, *partner_rest, taps_first, mid), scratch_in, PAIR_COST
    )
    next_edge = next_chip(edge_sum)

    def first_next(vol, wt, sum_ref, out, framed):
        out[...] = sum_ref[...] + spread(framed, vol[...], wt, (from_next,), 0)

    side = run(first_next, part, (beyond, taps_first, so_far), scratch_in)

    def hidden_own(*refs):
        vols, (wt, side_ref, b, top, low, framed) = refs[: nc - 1], refs[nc - 1 :]
        total = side_ref[...]
        for vol, k in zip(vols, others):
            total += spread(framed, vol[...], wt, (from_next,), k)
        cells = jnp.maximum(total + b[...], 0.0).astype(BF16)
        top[...] = cells[: hw // 2]
        low[...] = cells[hw // 2 :]

    half_rows = sds((hw // 2, ob), BF16)
    hidden = run(hidden_own, [half_rows, half_rows], (*beyond_rest, taps_first, side, b_first), scratch_in)
    pair_hidden = [in_chip(x) for x in hidden]

    def second_own(top, low, wt, out, framed):
        lay_columns(jnp.concatenate([top[...], low[...]], axis=0).astype(F32), framed, h, w)
        out[...] = nine_taps(framed, depth_taps(1, wt), h, w)

    scratch_mid = [pltpu.VMEM(framed_mid.shape, BF16)]
    whole = sds((hw, full), F32)
    second = run(second_own, whole, (*hidden, w_second), scratch_mid)
    def wanted(k):
        owner = lax.rem(lax.axis_index("chan") + k, nc)
        return pl.ds(pl.multiple_of(owner * own_out, own_out), own_out)

    def taps_for(wt, where, k):
        if own_out % 128 == 0:
            return wt[pl.ds(where * 9, 9), :, wanted(k)]
        owner = lax.rem(lax.axis_index("chan") + k, nc)
        taps = wt[pl.ds(where * 9, 9)]
        picked = taps[:, :, 0:own_out]
        for i in range(1, nc):
            picked = jnp.where(owner == i, taps[:, :, i * own_out : (i + 1) * own_out], picked)
        return picked

    def columns_for(ref, rows, k):
        if own_out % 128 == 0:
            return ref[rows, wanted(k)]
        owner = lax.rem(lax.axis_index("chan") + k, nc)
        cells = ref[rows]
        picked = cells[:, 0:own_out]
        for i in range(1, nc):
            picked = jnp.where(owner == i, cells[:, i * own_out : (i + 1) * own_out], picked)
        return picked

    def beside_rows(top, low, edge, mine, b, wt, before, frames, ks, start, stop):
        first, last = max(start - 1, 0), min(stop + 1, h)
        rows = slice(first * w, last * w)
        count = last - first
        pair_cells = jnp.concatenate([top[...], low[...]], axis=0)[rows].astype(F32)
        place = lax.axis_index("space")
        inside = jnp.logical_and(place > 0, place < ns - 1)
        total = edge[rows].astype(F32) + mine[rows] + b[...]
        edge_cells = jnp.where(inside, jnp.maximum(total, 0.0), 0.0)
        lay_columns(pair_cells, frames.at[0], count, w)
        lay_columns(edge_cells, frames.at[1], count, w)
        skip = start - first
        out = []
        for k in ks:
            sums = columns_for(before, slice(start * w, stop * w), k)
            taps = taps_for(wt, 2 - 2 * odd(), k)
            sums += nine_taps(frames.at[0], taps, stop - start, w, skip)
            taps = taps_for(wt, 2 * odd(), k)
            sums += nine_taps(frames.at[1], taps, stop - start, w, skip)
            out.append(sums)
        return out

    def send_rows(start, stop):
        def kernel(*refs):
            ins, outs, frames = refs[:7], refs[7:-1], refs[-1]
            for out, sums in zip(outs, beside_rows(*ins, frames, others, start, stop)):
                out[...] = sums.astype(BF16)

        return kernel

    two_frames = [pltpu.VMEM((2, (h + 2) * w, 3 * ob), BF16)]
    beside_in = (*pair_hidden, next_edge, onward, b_first, w_second, second)
    chunks = [(0, h // 2), (h // 2, h)]
    parts = []
    for start, stop in chunks:
        sends = run(
            send_rows(start, stop),
            [sds(((stop - start) * w, own_out), BF16)] * (nc - 1),
            beside_in,
            two_frames,
        )
        parts.append([round_chan(sends[k - 1], k) for k in others])

    def second_keep(*refs):
        ins, (b, out, frames) = refs[:7], refs[7:]
        out[...] = beside_rows(*ins, frames, [0], 0, h)[0] + b[...]

    kept = run(
        second_keep,
        sds((hw, own_out), F32),
        (*beside_in, b_second),
        two_frames,
        flops=36 * hw * ob * own_out,
    )

    def finish(kept_ref, *refs):
        total, out = kept_ref[...], refs[-1]
        for k in range(nc - 1):
            pieces_in = [refs[i * (nc - 1) + k][...] for i in range(len(chunks))]
            total += jnp.concatenate(pieces_in, axis=0).astype(F32)
        out[...] = channels_first(jnp.maximum(total, 0.0), h, w).astype(BF16)

    result = run(
        finish,
        sds((own_out, h, w), BF16),
        (kept, *[x for part in parts for x in part]),
        flops=2 * hw * own_out,
    )
    return result.reshape(own_out, 1, h, w)


def solution(mesh):
    in_specs = (
        P("chan", "space", None, None),
        P(None, None, "chan"),
        P("chan"),
        P("chan", None, None),
        P("chan"),
    )
    return jax.shard_map(
        functools.partial(per_device, mesh.shape["space"], mesh.shape["chan"]),
        mesh=mesh,
        in_specs=in_specs,
        out_specs=P("chan", "space", None, None),
        check_vma=False,
    )
```
